32 devices in a mesh: lon: 8 (over z, y), rad: 4 (over x, core).
Axes of the slice: x: 2, y: 2, z: 4, core: 2. Of those that a mesh axis runs over, the one named last changes fastest.
Arguments:
- adjoint_temp: float32 [32, 256, 128], P('rad', 'lon'), may hold values from -6 to 6
- viscosity: float32 [32, 256, 128], P('rad', 'lon'), may hold values from 0.1 to 10
- velocity: float32 [3, 32, 256, 128], P(None, 'rad', 'lon'), may hold values from -6 to 6
- misfit_force: float32 [3, 32, 256, 128], P(None, 'rad', 'lon'), may hold values from -6 to 6
- adjoint_guess: float32 [3, 32, 256, 128], P(None, 'rad', 'lon'), may hold values from -3 to 3
Outputs:
- temp_next: float32 [32, 256, 128], P('rad', 'lon')
- adjoint_vel: float32 [3, 32, 256, 128], P(None, 'rad', 'lon')
The draws below stay inside these ranges and needn't reach their ends.
All inputs are finite; a program needn't handle non-finite values.
Results may differ from the reference program's by a relative error of at most 0.00002.
Values sent between devices are 32-bit elements; how exact they have to be, the bound alone decides.
A program may use at most 128 MiB of HBM per device.

```python
import math
import jax
import jax.numpy as jnp

LAT = 128
NU = 2
NC = 8
NR = 32
NL = 256


def block_scale(own_key, dims, shards, least, largest):
    loudness = 1.0
    for axis_at, shards_of in shards:
        steps = jax.random.uniform(jax.random.fold_in(jax.random.fold_in(own_key, 6), axis_at), (shards_of,), jnp.float32, least / len(shards), largest / len(shards))
        loudness = loudness * jnp.repeat(jnp.exp(steps), dims[axis_at] // shards_of).reshape((-1,) + (1,) * (len(dims) - 1 - axis_at))
    return loudness


def bell_draw(key, shape, scale, bound, pieces=(), kind=jnp.bfloat16):
    level = block_scale(key, shape, pieces, -0.22, 0.18) if pieces else 1.0
    result = jax.random.normal(key, shape, jnp.float32) * scale * level
    return jnp.minimum(jnp.maximum(result, -bound), bound).astype(kind)


def setup_inputs(seed: int = 0) -> dict:
    streams_of = jax.random.split(jax.random.key(seed), 6)
    return {
        "adjoint_temp": bell_draw(streams_of[0], (NR, NL, LAT), 1.0, 6.0, ((0, 4), (1, 8)), jnp.float32),
        "viscosity": jnp.clip(jnp.exp(math.log(10.0) - 4.6051702 * jax.random.uniform(streams_of[1], (NR, NL, LAT), jnp.float32) ** block_scale(streams_of[1], (NR, NL, LAT), ((0, 4), (1, 8)), -0.2, 0.2)), 0.1, 10.0),
        "velocity": bell_draw(streams_of[2], (3, NR, NL, LAT), 1.0, 6.0, ((1, 4), (2, 8)), jnp.float32),
        "misfit_force": bell_draw(streams_of[3], (3, NR, NL, LAT), 1.0, 6.0, ((1, 4), (2, 8)), jnp.float32),
        "adjoint_guess": bell_draw(streams_of[4], (3, NR, NL, LAT), 0.5, 3.0, ((1, 4), (2, 8)), jnp.float32),
    }


def shift_zero(x, axis, lower):
    size = x.shape[axis]
    zero = jnp.zeros_like(jax.lax.slice_in_dim(x, 0, 1, axis=axis))
    if lower:
        return jnp.concatenate([zero, jax.lax.slice_in_dim(x, 0, size - 1, axis=axis)], axis=axis)
    return jnp.concatenate([jax.lax.slice_in_dim(x, 1, size, axis=axis), zero], axis=axis)


def neighbours(x):
    west = jnp.roll(x, 1, axis=2)
    east = jnp.roll(x, -1, axis=2)
    down = shift_zero(x, 1, True)
    upper = shift_zero(x, 1, False)
    south = shift_zero(x, 3, True)
    north = shift_zero(x, 3, False)
    return [west, east, down, upper, south, north]


def face_coefs(visc, near):
    coefs = [(visc + item) * 0.5 for item in near]
    diag = coefs[0] + coefs[1] + coefs[2] + coefs[3] + coefs[4] + coefs[5]
    return coefs, diag


def apply_op(field, coefs, diag, scale):
    near = neighbours(field)
    total = coefs[0] * near[0] + coefs[1] * near[1] + coefs[2] * near[2]
    total = total + coefs[3] * near[3] + coefs[4] * near[4] + coefs[5] * near[5]
    return scale * (diag * field - total)


def restrict(x):
    comps, rows, cols, width = x.shape
    return x.reshape(comps, rows // 2, 2, cols // 2, 2, width // 2, 2).mean(axis=(2, 4, 6))


def prolong(x):
    return jnp.repeat(jnp.repeat(jnp.repeat(x, 2, axis=1), 2, axis=2), 2, axis=3)


def reference(adjoint_temp, viscosity, velocity, misfit_force, adjoint_guess):
    both = jnp.stack([adjoint_temp, viscosity])
    near = neighbours(both)
    temp = both[0]
    tn = [item[0] for item in near]
    advect = velocity[0] * (tn[3] - tn[2]) + velocity[1] * (tn[1] - tn[0]) + velocity[2] * (tn[5] - tn[4])
    spread = tn[0] + tn[1] + tn[2] + tn[3] + tn[4] + tn[5] - 6.0 * temp
    temp_next = temp + 0.25 * advect * 0.5 + 0.1 * spread
    visc = both[1:2]
    coefs, diag = face_coefs(visc, [item[1:2] for item in near])
    rhs = misfit_force.at[0].add(temp_next)
    field = adjoint_guess
    for sweep in range(NU):
        field = field + 0.8 * (rhs - apply_op(field, coefs, diag, 1.0)) / diag
    coarse_res = restrict(rhs - apply_op(field, coefs, diag, 1.0))
    coarse_visc = restrict(visc)
    ccoefs, cdiag = face_coefs(coarse_visc, neighbours(coarse_visc))
    corr = jnp.zeros_like(coarse_res)
    for sweep in range(NC):
        corr = corr + 0.8 * (coarse_res - apply_op(corr, ccoefs, cdiag, 0.25)) / (0.25 * cdiag)
    field = field + prolong(corr)
    for sweep in range(NU):
        field = field + 0.8 * (rhs - apply_op(field, coefs, diag, 1.0)) / diag
    return temp_next, field
```

```python
import functools

import jax
import jax.numpy as jnp
from jax import lax
from jax.experimental import pallas as pl
from jax.experimental.pallas import tpu as pltpu
from jax.sharding import PartitionSpec as P

NU = 2
NC = 8
PAD = 8
MESH = pl.DeviceIdType.MESH


def kernel(ni, nj, temp_ref, visc_ref, vel_ref, mis_ref, guess_ref, tn_ref, out_ref,
           W0, U1, U2, U3, U4, WT, B, D, RS, CP, CV, G, CG, CW, CB, EA, EB, EX,
           S0, L0, S, L, send, recv):
    R, C, LAT = temp_ref.shape
    half = R // 4
    cols = C // 2
    strip = PAD
    i = lax.axis_index("lon")
    j = lax.axis_index("rad")
    west, east = lax.rem(i + ni - 1, ni), lax.rem(i + 1, ni)
    down, up = lax.rem(j + nj - 1, nj), lax.rem(j + 1, nj)

    barrier = pltpu.get_barrier_semaphore()
    for d in range(nj):
        other = lax.rem(j + d, nj)
        for lon in (west, east) if d == 0 else (west, east, i):
            pl.semaphore_signal(barrier, inc=1, device_id={"lon": lon, "rad": other}, device_id_type=MESH)

    mid = pl.ds(PAD, C)
    lane = lax.broadcasted_iota(jnp.int32, (C, LAT), 1)
    first, last = lane == 0, lane == LAT - 1
    even = lax.rem(lane, 2) == 0
    even_half = even[:cols]

    W0[0:3, 1 : R + 1, PAD : PAD + C, :] = guess_ref[...]
    W0[3, 1 : R + 1, PAD : PAD + C, :] = temp_ref[...]
    W0[4, 1 : R + 1, PAD : PAD + C, :] = visc_ref[...]

    def pack(slot, dst):
        for r in range(half):
            a = RS[slot, r, pl.ds(0, cols, 2), :] + RS[slot, r, pl.ds(1, cols, 2), :]
            b = RS[slot, r + half, pl.ds(0, cols, 2), :] + RS[slot, r + half, pl.ds(1, cols, 2), :]
            a = a + pltpu.roll(a, LAT - 1, 1)
            b = b + pltpu.roll(b, 1, 1)
            dst[r] = 0.125 * jnp.where(even_half, a, b)

    for q in range(2 * half):
        RS[3, q] = visc_ref[2 * q] + visc_ref[2 * q + 1]
    pack(3, CV.at[0])

    def copy(src, dst, slot, lon, rad):
        return pltpu.make_async_remote_copy(
            src_ref=src, dst_ref=dst, send_sem=send.at[slot], recv_sem=recv.at[slot],
            device_id={"lon": lon, "rad": rad}, device_id_type=MESH)

    pending = []

    def begin(slot, buf, stage, land, comps):
        for c in range(comps):
            stage[0, c] = buf[c, 1 : R + 1, PAD, :]
            stage[1, c] = buf[c, 1 : R + 1, PAD + C - 1, :]
        copies = [
            copy(stage.at[0], land.at[1], slot, west, j),
            copy(stage.at[1], land.at[0], slot + 1, east, j),
            copy(buf.at[:, 1, mid], buf.at[:, R + 1, mid], slot + 2, i, down),
            copy(buf.at[:, R, mid], buf.at[:, 0, mid], slot + 3, i, up),
        ]
        for item in copies:
            item.start()
        pending.extend(copies)
        return copies

    def finish(copies, buf, land, comps):
        for item in copies:
            item.wait_recv()
        for c in range(comps):
            buf[c, 1 : R + 1, PAD - 1, :] = land[0, c]
            buf[c, 1 : R + 1, PAD + C, :] = land[1, c]

    gathers = 3 * nj - 1

    def gather(slot, src, dst, width):
        copies = []
        rows = pl.ds(1 + half * j, half)
        for d in range(nj):
            other = lax.rem(j + d, nj)
            copies.append(copy(src.at[:, :, pl.ds(0, width)], dst.at[:, rows, pl.ds(2 * strip + cols, width)], slot, west, other))
            copies.append(copy(src.at[:, :, pl.ds(cols - width, width)], dst.at[:, rows, pl.ds(2 * strip - width, width)], slot + 1, east, other))
            slot = slot + 2
            if d > 0:
                copies.append(copy(src, dst.at[:, rows, pl.ds(2 * strip, cols)], slot, i, other))
                slot = slot + 1
        for item in copies:
            item.start()
        pending.extend(copies)
        for r in range(half):
            dst[:, 1 + half * j + r, 2 * strip : 2 * strip + cols, :] = src[:, r]
        return copies

    top = half * nj + 1
    for buf in (EA, EB):
        buf[...] = jnp.zeros_like(buf)
    CG[0, 0] = jnp.zeros_like(CG[0, 0])
    CG[0, top] = jnp.zeros_like(CG[0, top])

    pl.semaphore_wait(barrier, gathers)

    round0 = begin(0, W0, S0, L0, 5)
    coarse_visc = gather(16, CV, CG, cols)
    finish(round0, W0, L0, 5)

    @pl.when(j == 0)
    def _():
        W0[3:5, 0] = jnp.zeros_like(W0[3:5, 0])

    @pl.when(j == nj - 1)
    def _():
        W0[3:5, R + 1] = jnp.zeros_like(W0[3:5, R + 1])

    def near(buf, c, r):
        x = buf[c, r + 1, PAD : PAD + C, :]
        return x, [
            buf[c, r + 1, PAD - 1 : PAD + C - 1, :],
            buf[c, r + 1, PAD + 1 : PAD + C + 1, :],
            buf[c, r, PAD : PAD + C, :],
            buf[c, r + 2, PAD : PAD + C, :],
            pltpu.roll(x, 1, 1),
            pltpu.roll(x, LAT - 1, 1),
        ]

    def setup(r, carry):
        v, vn = near(W0, 4, r)
        vn[4] = jnp.where(first, 0.0, vn[4])
        vn[5] = jnp.where(last, 0.0, vn[5])
        coefs = [(v + item) * 0.5 for item in vn]
        diag = coefs[0] + coefs[1] + coefs[2] + coefs[3] + coefs[4] + coefs[5]
        inv = 0.8 / diag
        coefs[4] = jnp.where(first, 0.0, coefs[4])
        coefs[5] = jnp.where(last, 0.0, coefs[5])
        for k in range(6):
            WT[k, r] = coefs[k] * inv
        D[r] = diag * 1.25
        t, tn = near(W0, 3, r)
        tn[4] = jnp.where(first, 0.0, tn[4])
        tn[5] = jnp.where(last, 0.0, tn[5])
        advect = vel_ref[0, r] * (tn[3] - tn[2]) + vel_ref[1, r] * (tn[1] - tn[0]) + vel_ref[2, r] * (tn[5] - tn[4])
        spread = tn[0] + tn[1] + tn[2] + tn[3] + tn[4] + tn[5] - 6.0 * t
        t_next = t + 0.125 * advect + 0.1 * spread
        tn_ref[r] = t_next
        B[0, r] = (mis_ref[0, r] + t_next) * inv
        B[1, r] = mis_ref[1, r] * inv
        B[2, r] = mis_ref[2, r] * inv
        return carry

    lax.fori_loop(0, R, setup, 0)

    @pl.when(j == 0)
    def _():
        WT[2, 0] = jnp.zeros_like(WT[2, 0])

    @pl.when(j == nj - 1)
    def _():
        WT[3, R - 1] = jnp.zeros_like(WT[3, R - 1])

    def change(buf, c, r):
        x, xn = near(buf, c, r)
        t = B[c, r] - 0.8 * x
        for k in range(6):
            t = t + WT[k, r] * xn[k]
        return x, t

    def sweep(src, dst):
        def body(r, carry):
            for c in range(3):
                x, t = change(src, c, r)
                dst[c, r + 1, PAD : PAD + C, :] = x + t
            return carry

        lax.fori_loop(0, R, body, 0)

    sweep(W0, U1)
    round1 = begin(4, U1, S.at[0], L.at[0], 3)

    for item in coarse_visc:
        item.wait_recv()

    def coarse_near(buf, c, at, r):
        p = 1 + half * at + r
        x = buf[c, p, PAD : PAD + C, :]
        if r > 0:
            below = buf[c, p - 1, PAD : PAD + C, :]
        else:
            below = jnp.where(even, pltpu.roll(buf[c, p - 1, PAD : PAD + C, :], LAT - 1, 1),
                              pltpu.roll(buf[c, p + half - 1, PAD : PAD + C, :], 1, 1))
        if r < half - 1:
            above = buf[c, p + 1, PAD : PAD + C, :]
        else:
            above = jnp.where(even, pltpu.roll(buf[c, p - half + 1, PAD : PAD + C, :], LAT - 1, 1),
                              pltpu.roll(buf[c, p + 1, PAD : PAD + C, :], 1, 1))
        return x, [
            buf[c, p, PAD - 1 : PAD + C - 1, :],
            buf[c, p, PAD + 1 : PAD + C + 1, :],
            below,
            above,
            pltpu.roll(x, 2, 1),
            pltpu.roll(x, LAT - 2, 1),
        ]

    def coarse_setup(at, carry):
        for r in range(half):
            v, vn = coarse_near(CG, 0, at, r)
            vn[4] = jnp.where(lane < 2, 0.0, vn[4])
            vn[5] = jnp.where(lane >= LAT - 2, 0.0, vn[5])
            coefs = [(v + item) * 0.5 for item in vn]
            diag = coefs[0] + coefs[1] + coefs[2] + coefs[3] + coefs[4] + coefs[5]
            inv = 0.8 / diag
            coefs[4] = jnp.where(lane < 2, 0.0, coefs[4])
            coefs[5] = jnp.where(lane >= LAT - 2, 0.0, coefs[5])
            for k in range(6):
                CW[k, half * at + r] = coefs[k] * inv
            CW[6, half * at + r] = 4.0 * inv
        return carry

    lax.fori_loop(0, nj, coarse_setup, 0)

    finish(round1, U1, L.at[0], 3)
    sweep(U1, U2)
    round2 = begin(8, U2, S.at[1], L.at[1], 3)
    finish(round2, U2, L.at[1], 3)

    def residual(q, carry):
        for c in range(3):
            total = D[2 * q] * change(U2, c, 2 * q)[1]
            RS[c, q] = total + D[2 * q + 1] * change(U2, c, 2 * q + 1)[1]
        return carry

    lax.fori_loop(0, 2 * half, residual, 0)
    for c in range(3):
        pack(c, CP.at[c])
    coarse_res = gather(16 + gathers, CP, G, strip)
    for item in coarse_res:
        item.wait_recv()

    def coarse_first(p, carry):
        for c in range(3):
            b = G[c, p + 1, PAD : PAD + C, :] * CW[6, p]
            CB[c, p] = b
            EA[c, p + 1, PAD : PAD + C, :] = b
        return carry

    lax.fori_loop(0, half * nj, coarse_first, 0)

    def coarse_sweep(src, dst):
        def body(at, carry):
            for r in range(half):
                p = half * at + r
                for c in range(3):
                    x, xn = coarse_near(src, c, at, r)
                    t = CB[c, p] + 0.2 * x
                    for k in range(6):
                        t = t + CW[k, p] * xn[k]
                    dst[c, p + 1, PAD : PAD + C, :] = t
            return carry

        lax.fori_loop(0, nj, body, 0)

    src, dst = EA, EB
    for number in range(NC - 1):
        coarse_sweep(src, dst)
        src, dst = dst, src

    wide = EX.shape[2] // 2
    start = 2 * strip - PAD // 2
    even_wide = lax.rem(lax.broadcasted_iota(jnp.int32, (wide, LAT), 1), 2) == 0
    for c in range(3):
        for q in range(-1, 2 * half + 1):
            low = 0 <= q < half or q == 2 * half
            place = 1 + half * j + {-1: -1, 2 * half: half}.get(q, q % half)
            x = src[c, place, start : start + wide, :]
            if low:
                x = jnp.where(even_wide, x, pltpu.roll(x, 1, 1))
            else:
                x = jnp.where(even_wide, pltpu.roll(x, LAT - 1, 1), x)
            EX[c, q + 1, pl.ds(0, wide, 2), :] = x
            EX[c, q + 1, pl.ds(1, wide, 2), :] = x
    for c in range(3):
        for r in range(-1, R + 1):
            U3[c, r + 1] = U2[c, r + 1] + EX[c, r // 2 + 1]

    sweep(U3, U4)
    round3 = begin(12, U4, S.at[2], L.at[2], 3)
    finish(round3, U4, L.at[2], 3)

    def closing(r, carry):
        for c in range(3):
            x, t = change(U4, c, r)
            out_ref[c, r] = x + t
        return carry

    lax.fori_loop(0, R, closing, 0)
    for item in pending:
        item.wait_send()


def solution(mesh):
    ni, nj = mesh.shape["lon"], mesh.shape["rad"]

    def local(adjoint_temp, viscosity, velocity, misfit_force, adjoint_guess):
        R, C, LAT = adjoint_temp.shape
        half, cols, wide = R // 4, C // 2, C + 2 * PAD
        f32 = jnp.float32
        frame = lambda n, rows: pltpu.VMEM((n, rows, wide, LAT), f32)
        block = lambda *dims: pltpu.VMEM(dims + (C, LAT), f32)
        copies = 16 + 2 * (3 * nj - 1)
        vmem = pl.BlockSpec(memory_space=pltpu.VMEM)
        P8 = half * nj
        return pl.pallas_call(
            functools.partial(kernel, ni, nj),
            out_shape=(
                jax.ShapeDtypeStruct(adjoint_temp.shape, f32),
                jax.ShapeDtypeStruct(adjoint_guess.shape, f32),
            ),
            in_specs=[vmem] * 5,
            out_specs=(vmem, vmem),
            scratch_shapes=[
                frame(5, R + 2), frame(3, R + 2), frame(3, R + 2), frame(3, R + 2), frame(3, R + 2),
                block(6, R), block(3, R), block(R), block(4, 2 * half),
                pltpu.VMEM((3, half, cols, LAT), f32), pltpu.VMEM((1, half, cols, LAT), f32),
                frame(3, P8 + 2), frame(1, P8 + 2), block(7, P8), block(3, P8),
                frame(3, P8 + 2), frame(3, P8 + 2), frame(3, 2 * half + 2),
                pltpu.VMEM((2, 5, R, LAT), f32), pltpu.VMEM((2, 5, R, LAT), f32),
                pltpu.VMEM((3, 2, 3, R, LAT), f32), pltpu.VMEM((3, 2, 3, R, LAT), f32),
                pltpu.SemaphoreType.DMA((copies,)), pltpu.SemaphoreType.DMA((copies,)),
            ],
            compiler_params=pltpu.CompilerParams(collective_id=0, has_side_effects=True),
        )(adjoint_temp, viscosity, velocity, misfit_force, adjoint_guess)

    flat = P("rad", "lon", None)
    full = P(None, "rad", "lon", None)
    return jax.shard_map(local, mesh=mesh, in_specs=(flat, flat, full, full, full), out_specs=(flat, full), check_vma=False)
```

```python
import functools

import jax
import jax.numpy as jnp
from jax import lax
from jax.experimental import pallas as pl
from jax.experimental.pallas import tpu as pltpu
from jax.sharding import PartitionSpec as P

NU = 2
NC = 8
PAD = 8
MESH = pl.DeviceIdType.MESH


def kernel(ni, nj, temp_hbm, visc_hbm, vel_hbm, mis_hbm, guess_hbm, tn_ref, out_ref,
           vel_ref, mis_ref, local,
           W0, U1, U2, U3, U4, WT, B, D, RS, CP, CV, G, CG, CW, CB, EA, EB, EX,
           S0, L0, S, L, send, recv):
    R, C, LAT = temp_hbm.shape
    half = R // 4
    cols = C // 2
    strip = PAD
    i = lax.axis_index("lon")
    j = lax.axis_index("rad")
    west, east = lax.rem(i + ni - 1, ni), lax.rem(i + 1, ni)
    down, up = lax.rem(j + nj - 1, nj), lax.rem(j + 1, nj)

    mid = pl.ds(PAD, C)
    inner = pl.ds(1, R)
    loads = [
        pltpu.make_async_copy(visc_hbm, W0.at[4, inner, mid], local.at[0]),
        pltpu.make_async_copy(temp_hbm, W0.at[3, inner, mid], local.at[1]),
        pltpu.make_async_copy(guess_hbm, W0.at[0:3, inner, mid], local.at[2]),
        pltpu.make_async_copy(vel_hbm, vel_ref, local.at[3]),
        pltpu.make_async_copy(mis_hbm, mis_ref, local.at[4]),
    ]
    for item in loads:
        item.start()

    barrier = pltpu.get_barrier_semaphore()
    for d in range(nj):
        other = lax.rem(j + d, nj)
        for lon in (west, east) if d == 0 else (west, east, i):
            pl.semaphore_signal(barrier, inc=1, device_id={"lon": lon, "rad": other}, device_id_type=MESH)

    lane = lax.broadcasted_iota(jnp.int32, (C, LAT), 1)
    first, last = lane == 0, lane == LAT - 1
    even = lax.rem(lane, 2) == 0
    even_half = even[:cols]

    def pack(slot, dst):
        for r in range(half):
            a = RS[slot, r, pl.ds(0, cols, 2), :] + RS[slot, r, pl.ds(1, cols, 2), :]
            b = RS[slot, r + half, pl.ds(0, cols, 2), :] + RS[slot, r + half, pl.ds(1, cols, 2), :]
            a = a + pltpu.roll(a, LAT - 1, 1)
            b = b + pltpu.roll(b, 1, 1)
            dst[r] = 0.125 * jnp.where(even_half, a, b)


    def copy(src, dst, slot, lon, rad):
        return pltpu.make_async_remote_copy(
            src_ref=src, dst_ref=dst, send_sem=send.at[slot], recv_sem=recv.at[slot],
            device_id={"lon": lon, "rad": rad}, device_id_type=MESH)

    pending = []

    def begin(slot, buf, stage, land, comps):
        for c in range(comps):
            stage[0, c] = buf[c, 1 : R + 1, PAD, :]
            stage[1, c] = buf[c, 1 : R + 1, PAD + C - 1, :]
        copies = [
            copy(stage.at[0], land.at[1], slot, west, j),
            copy(stage.at[1], land.at[0], slot + 1, east, j),
            copy(buf.at[:, 1, mid], buf.at[:, R + 1, mid], slot + 2, i, down),
            copy(buf.at[:, R, mid], buf.at[:, 0, mid], slot + 3, i, up),
        ]
        for item in copies:
            item.start()
        pending.extend(copies)
        return copies

    def finish(copies, buf, land, comps):
        for item in copies:
            item.wait_recv()
        for c in range(comps):
            buf[c, 1 : R + 1, PAD - 1, :] = land[0, c]
            buf[c, 1 : R + 1, PAD + C, :] = land[1, c]

    gathers = 3 * nj - 1

    def gather(slot, src, dst, width):
        copies = []
        rows = pl.ds(1 + half * j, half)
        for d in range(nj):
            other = lax.rem(j + d, nj)
            copies.append(copy(src.at[:, :, pl.ds(0, width)], dst.at[:, rows, pl.ds(2 * strip + cols, width)], slot, west, other))
            copies.append(copy(src.at[:, :, pl.ds(cols - width, width)], dst.at[:, rows, pl.ds(2 * strip - width, width)], slot + 1, east, other))
            slot = slot + 2
            if d > 0:
                copies.append(copy(src, dst.at[:, rows, pl.ds(2 * strip, cols)], slot, i, other))
                slot = slot + 1
        for item in copies:
            item.start()
        pending.extend(copies)
        for r in range(half):
            dst[:, 1 + half * j + r, 2 * strip : 2 * strip + cols, :] = src[:, r]
        return copies

    top = half * nj + 1
    for buf in (EA, EB):
        buf[...] = jnp.zeros_like(buf)
    CG[0, 0] = jnp.zeros_like(CG[0, 0])
    CG[0, top] = jnp.zeros_like(CG[0, top])

    loads[0].wait()
    for q in range(2 * half):
        RS[3, q] = W0[4, 2 * q + 1, PAD : PAD + C, :] + W0[4, 2 * q + 2, PAD : PAD + C, :]
    pack(3, CV.at[0])
    loads[1].wait()
    loads[2].wait()
    pl.semaphore_wait(barrier, gathers)

    round0 = begin(0, W0, S0, L0, 5)
    coarse_visc = gather(16, CV, CG, cols)
    loads[3].wait()
    loads[4].wait()
    finish(round0, W0, L0, 5)

    @pl.when(j == 0)
    def _():
        W0[3:5, 0] = jnp.zeros_like(W0[3:5, 0])

    @pl.when(j == nj - 1)
    def _():
        W0[3:5, R + 1] = jnp.zeros_like(W0[3:5, R + 1])

    def near(buf, c, r):
        x = buf[c, r + 1, PAD : PAD + C, :]
        return x, [
            buf[c, r + 1, PAD - 1 : PAD + C - 1, :],
            buf[c, r + 1, PAD + 1 : PAD + C + 1, :],
            buf[c, r, PAD : PAD + C, :],
            buf[c, r + 2, PAD : PAD + C, :],
            pltpu.roll(x, 1, 1),
            pltpu.roll(x, LAT - 1, 1),
        ]

    def setup(r, carry):
        v, vn = near(W0, 4, r)
        vn[4] = jnp.where(first, 0.0, vn[4])
        vn[5] = jnp.where(last, 0.0, vn[5])
        coefs = [(v + item) * 0.5 for item in vn]
        diag = coefs[0] + coefs[1] + coefs[2] + coefs[3] + coefs[4] + coefs[5]
        inv = 0.8 / diag
        coefs[4] = jnp.where(first, 0.0, coefs[4])
        coefs[5] = jnp.where(last, 0.0, coefs[5])
        for k in range(6):
            WT[k, r] = coefs[k] * inv
        D[r] = diag * 1.25
        t, tn = near(W0, 3, r)
        tn[4] = jnp.where(first, 0.0, tn[4])
        tn[5] = jnp.where(last, 0.0, tn[5])
        advect = vel_ref[0, r] * (tn[3] - tn[2]) + vel_ref[1, r] * (tn[1] - tn[0]) + vel_ref[2, r] * (tn[5] - tn[4])
        spread = tn[0] + tn[1] + tn[2] + tn[3] + tn[4] + tn[5] - 6.0 * t
        t_next = t + 0.125 * advect + 0.1 * spread
        tn_ref[r] = t_next
        B[0, r] = (mis_ref[0, r] + t_next) * inv
        B[1, r] = mis_ref[1, r] * inv
        B[2, r] = mis_ref[2, r] * inv
        return carry

    lax.fori_loop(0, R, setup, 0)

    @pl.when(j == 0)
    def _():
        WT[2, 0] = jnp.zeros_like(WT[2, 0])

    @pl.when(j == nj - 1)
    def _():
        WT[3, R - 1] = jnp.zeros_like(WT[3, R - 1])

    def change(buf, c, r):
        x, xn = near(buf, c, r)
        t = B[c, r] - 0.8 * x
        for k in range(6):
            t = t + WT[k, r] * xn[k]
        return x, t

    def sweep(src, dst):
        def body(r, carry):
            for c in range(3):
                x, t = change(src, c, r)
                dst[c, r + 1, PAD : PAD + C, :] = x + t
            return carry

        lax.fori_loop(0, R, body, 0)

    sweep(W0, U1)
    round1 = begin(4, U1, S.at[0], L.at[0], 3)

    for item in coarse_visc:
        item.wait_recv()

    def coarse_near(buf, c, at, r, lo=PAD, width=None):
        width = width or C
        part = even[:width]
        p = 1 + half * at + r
        block = lambda place, off=0: buf[c, place, lo + off : lo + off + width, :]
        x = block(p)
        if r > 0:
            below = block(p - 1)
        else:
            below = jnp.where(part, pltpu.roll(block(p - 1), LAT - 1, 1), pltpu.roll(block(p + half - 1), 1, 1))
        if r < half - 1:
            above = block(p + 1)
        else:
            above = jnp.where(part, pltpu.roll(block(p - half + 1), LAT - 1, 1), pltpu.roll(block(p + 1), 1, 1))
        return x, [block(p, -1), block(p, 1), below, above, pltpu.roll(x, 2, 1), pltpu.roll(x, LAT - 2, 1)]

    def coarse_setup(at, carry):
        for r in range(half):
            v, vn = coarse_near(CG, 0, at, r)
            vn[4] = jnp.where(lane < 2, 0.0, vn[4])
            vn[5] = jnp.where(lane >= LAT - 2, 0.0, vn[5])
            coefs = [(v + item) * 0.5 for item in vn]
            diag = coefs[0] + coefs[1] + coefs[2] + coefs[3] + coefs[4] + coefs[5]
            inv = 0.8 / diag
            coefs[4] = jnp.where(lane < 2, 0.0, coefs[4])
            coefs[5] = jnp.where(lane >= LAT - 2, 0.0, coefs[5])
            for k in range(6):
                CW[k, half * at + r] = coefs[k] * inv
            CW[6, half * at + r] = 4.0 * inv
        return carry

    lax.fori_loop(0, nj, coarse_setup, 0)

    finish(round1, U1, L.at[0], 3)
    sweep(U1, U2)
    round2 = begin(8, U2, S.at[1], L.at[1], 3)
    finish(round2, U2, L.at[1], 3)

    def residual(q, carry):
        for c in range(3):
            total = D[2 * q] * change(U2, c, 2 * q)[1]
            RS[c, q] = total + D[2 * q + 1] * change(U2, c, 2 * q + 1)[1]
        return carry

    lax.fori_loop(0, 2 * half, residual, 0)
    for c in range(3):
        pack(c, CP.at[c])
    coarse_res = gather(16 + gathers, CP, G, strip)
    for item in coarse_res:
        item.wait_recv()

    def coarse_first(p, carry):
        for c in range(3):
            b = G[c, p + 1, PAD : PAD + C, :] * CW[6, p]
            CB[c, p] = b
            EA[c, p + 1, PAD : PAD + C, :] = b
        return carry

    lax.fori_loop(0, half * nj, coarse_first, 0)

    def coarse_sweep(src, dst, rim):
        near_rim = 2 * rim <= PAD and cols % 8 == 0
        lo = 2 * strip - PAD // 2 if near_rim else PAD
        width = cols + PAD if near_rim else C
        reach = -(-rim // (2 * half))

        def body(at, carry):
            for r in range(half):
                p = half * at + r
                for c in range(3):
                    x, xn = coarse_near(src, c, at, r, lo, width)
                    t = CB[c, p, lo - PAD : lo - PAD + width, :] + 0.2 * x
                    for k in range(6):
                        t = t + CW[k, p, lo - PAD : lo - PAD + width, :] * xn[k]
                    dst[c, p + 1, lo : lo + width, :] = t
            return carry

        lax.fori_loop(jnp.maximum(j - reach, 0), jnp.minimum(j + reach + 1, nj), body, 0)

    src, dst = EA, EB
    for number in range(NC - 1):
        coarse_sweep(src, dst, NC - 1 - number)
        src, dst = dst, src

    wide = EX.shape[2] // 2
    start = 2 * strip - PAD // 2
    even_wide = lax.rem(lax.broadcasted_iota(jnp.int32, (wide, LAT), 1), 2) == 0
    for c in range(3):
        for q in range(-1, 2 * half + 1):
            low = 0 <= q < half or q == 2 * half
            place = 1 + half * j + {-1: -1, 2 * half: half}.get(q, q % half)
            x = src[c, place, start : start + wide, :]
            if low:
                x = jnp.where(even_wide, x, pltpu.roll(x, 1, 1))
            else:
                x = jnp.where(even_wide, pltpu.roll(x, LAT - 1, 1), x)
            EX[c, q + 1, pl.ds(0, wide, 2), :] = x
            EX[c, q + 1, pl.ds(1, wide, 2), :] = x
    for c in range(3):
        for r in range(-1, R + 1):
            U3[c, r + 1] = U2[c, r + 1] + EX[c, r // 2 + 1]

    sweep(U3, U4)
    round3 = begin(12, U4, S.at[2], L.at[2], 3)
    finish(round3, U4, L.at[2], 3)

    def closing(r, carry):
        for c in range(3):
            x, t = change(U4, c, r)
            out_ref[c, r] = x + t
        return carry

    lax.fori_loop(0, R, closing, 0)
    for item in pending:
        item.wait_send()


def deliver(tn_ref, out_ref, tn_hbm, out_hbm, sems):
    copies = [pltpu.make_async_copy(tn_ref, tn_hbm, sems.at[0]), pltpu.make_async_copy(out_ref, out_hbm, sems.at[1])]
    for item in copies:
        item.start()
    for item in copies:
        item.wait()


def solution(mesh):
    ni, nj = mesh.shape["lon"], mesh.shape["rad"]

    def local(adjoint_temp, viscosity, velocity, misfit_force, adjoint_guess):
        R, C, LAT = adjoint_temp.shape
        half, cols, wide = R // 4, C // 2, C + 2 * PAD
        f32 = jnp.float32
        frame = lambda n, rows: pltpu.VMEM((n, rows, wide, LAT), f32)
        block = lambda *dims: pltpu.VMEM(dims + (C, LAT), f32)
        copies = 16 + 2 * (3 * nj - 1)
        vmem, place = pl.BlockSpec(memory_space=pltpu.VMEM), pl.BlockSpec(memory_space=pl.ANY)
        P8 = half * nj
        results = pl.pallas_call(
            functools.partial(kernel, ni, nj),
            out_shape=(
                pltpu.VMEM(adjoint_temp.shape, f32),
                pltpu.VMEM(adjoint_guess.shape, f32),
            ),
            in_specs=[place] * 5,
            out_specs=(vmem, vmem),
            scratch_shapes=[
                block(3, R), block(3, R), pltpu.SemaphoreType.DMA((5,)),
                frame(5, R + 2), frame(3, R + 2), frame(3, R + 2), frame(3, R + 2), frame(3, R + 2),
                block(6, R), block(3, R), block(R), block(4, 2 * half),
                pltpu.VMEM((3, half, cols, LAT), f32), pltpu.VMEM((1, half, cols, LAT), f32),
                frame(3, P8 + 2), frame(1, P8 + 2), block(7, P8), block(3, P8),
                frame(3, P8 + 2), frame(3, P8 + 2), frame(3, 2 * half + 2),
                pltpu.VMEM((2, 5, R, LAT), f32), pltpu.VMEM((2, 5, R, LAT), f32),
                pltpu.VMEM((3, 2, 3, R, LAT), f32), pltpu.VMEM((3, 2, 3, R, LAT), f32),
                pltpu.SemaphoreType.DMA((copies,)), pltpu.SemaphoreType.DMA((copies,)),
            ],
            compiler_params=pltpu.CompilerParams(collective_id=0, has_side_effects=True),
        )(adjoint_temp, viscosity, velocity, misfit_force, adjoint_guess)
        return pl.pallas_call(
            deliver,
            out_shape=(jax.ShapeDtypeStruct(adjoint_temp.shape, f32), jax.ShapeDtypeStruct(adjoint_guess.shape, f32)),
            in_specs=[vmem] * 2,
            out_specs=(place, place),
            scratch_shapes=[pltpu.SemaphoreType.DMA((2,))],
        )(*[pltpu.with_memory_space_constraint(item, pltpu.VMEM) for item in results])

    flat = P("rad", "lon", None)
    full = P(None, "rad", "lon", None)
    return jax.shard_map(local, mesh=mesh, in_specs=(flat, flat, full, full, full), out_specs=(flat, full), check_vma=False)
```

```python
import functools

import jax
import jax.numpy as jnp
from jax import lax
from jax.experimental import pallas as pl
from jax.experimental.pallas import tpu as pltpu
from jax.sharding import PartitionSpec as P

NU = 2
NC = 8
PAD = 8
MESH = pl.DeviceIdType.MESH


def kernel(ni, nj, temp_hbm, visc_hbm, vel_hbm, mis_hbm, guess_hbm, tn_ref, out_ref,
           vel_ref, mis_ref, local,
           W0, U1, U2, U3, U4, SW, LW, WT, B, D, RS, CP, CV, G, CG, CW, CB, EA, EB, EX,
           S0, L0, S, L, send, recv):
    R, C, LAT = temp_hbm.shape
    half = R // 4
    cols = C // 2
    strip = PAD
    i = lax.axis_index("lon")
    j = lax.axis_index("rad")
    west, east = lax.rem(i + ni - 1, ni), lax.rem(i + 1, ni)
    down, up = lax.rem(j + nj - 1, nj), lax.rem(j + 1, nj)

    mid = pl.ds(PAD, C)
    inner = pl.ds(1, R)
    loads = [
        pltpu.make_async_copy(visc_hbm, W0.at[4, inner, mid], local.at[0]),
        pltpu.make_async_copy(temp_hbm, W0.at[3, inner, mid], local.at[1]),
        pltpu.make_async_copy(guess_hbm, W0.at[0:3, inner, mid], local.at[2]),
        pltpu.make_async_copy(vel_hbm, vel_ref, local.at[3]),
        pltpu.make_async_copy(mis_hbm, mis_ref, local.at[4]),
    ]
    for item in loads:
        item.start()

    barrier = pltpu.get_barrier_semaphore()
    for d in range(nj):
        other = lax.rem(j + d, nj)
        for lon in (west, east) if d == 0 else (west, east, i):
            pl.semaphore_signal(barrier, inc=1, device_id={"lon": lon, "rad": other}, device_id_type=MESH)

    lane = lax.broadcasted_iota(jnp.int32, (C, LAT), 1)
    first, last = lane == 0, lane == LAT - 1
    even = lax.rem(lane, 2) == 0
    even_half = even[:cols]

    def pack(slot, dst):
        for r in range(half):
            a = RS[slot, r, pl.ds(0, cols, 2), :] + RS[slot, r, pl.ds(1, cols, 2), :]
            b = RS[slot, r + half, pl.ds(0, cols, 2), :] + RS[slot, r + half, pl.ds(1, cols, 2), :]
            a = a + pltpu.roll(a, LAT - 1, 1)
            b = b + pltpu.roll(b, 1, 1)
            dst[r] = 0.125 * jnp.where(even_half, a, b)


    def copy(src, dst, slot, lon, rad):
        return pltpu.make_async_remote_copy(
            src_ref=src, dst_ref=dst, send_sem=send.at[slot], recv_sem=recv.at[slot],
            device_id={"lon": lon, "rad": rad}, device_id_type=MESH)

    pending = []

    def begin(slot, buf, stage, land, comps):
        for c in range(comps):
            stage[0, c] = buf[c, 1 : R + 1, PAD, :]
            stage[1, c] = buf[c, 1 : R + 1, PAD + C - 1, :]
        copies = [
            copy(stage.at[0], land.at[1], slot, west, j),
            copy(stage.at[1], land.at[0], slot + 1, east, j),
            copy(buf.at[:, 1, mid], buf.at[:, R + 1, mid], slot + 2, i, down),
            copy(buf.at[:, R, mid], buf.at[:, 0, mid], slot + 3, i, up),
        ]
        for item in copies:
            item.start()
        pending.extend(copies)
        return copies

    def finish(copies, buf, land, comps):
        for item in copies:
            item.wait_recv()
        for c in range(comps):
            buf[c, 1 : R + 1, PAD - 1, :] = land[0, c]
            buf[c, 1 : R + 1, PAD + C, :] = land[1, c]

    gathers = 3 * nj - 1

    def gather(slot, src, dst, width):
        copies = []
        rows = pl.ds(1 + half * j, half)
        for d in range(nj):
            other = lax.rem(j + d, nj)
            copies.append(copy(src.at[:, :, pl.ds(0, width)], dst.at[:, rows, pl.ds(2 * strip + cols, width)], slot, west, other))
            copies.append(copy(src.at[:, :, pl.ds(cols - width, width)], dst.at[:, rows, pl.ds(2 * strip - width, width)], slot + 1, east, other))
            slot = slot + 2
            if d > 0:
                copies.append(copy(src, dst.at[:, rows, pl.ds(2 * strip, cols)], slot, i, other))
                slot = slot + 1
        for item in copies:
            item.start()
        pending.extend(copies)
        for r in range(half):
            dst[:, 1 + half * j + r, 2 * strip : 2 * strip + cols, :] = src[:, r]
        return copies

    top = half * nj + 1
    for buf in (EA, EB):
        buf[...] = jnp.zeros_like(buf)
    CG[0, 0] = jnp.zeros_like(CG[0, 0])
    CG[0, top] = jnp.zeros_like(CG[0, top])

    loads[0].wait()
    for q in range(2 * half):
        RS[3, q] = W0[4, 2 * q + 1, PAD : PAD + C, :] + W0[4, 2 * q + 2, PAD : PAD + C, :]
    pack(3, CV.at[0])
    loads[1].wait()
    loads[2].wait()
    pl.semaphore_wait(barrier, gathers)

    round0 = begin(0, W0, S0, L0, 5)
    coarse_visc = gather(20, CV, CG, cols)
    loads[3].wait()
    loads[4].wait()
    finish(round0, W0, L0, 5)

    @pl.when(j == 0)
    def _():
        W0[3:5, 0] = jnp.zeros_like(W0[3:5, 0])

    @pl.when(j == nj - 1)
    def _():
        W0[3:5, R + 1] = jnp.zeros_like(W0[3:5, R + 1])

    def near(buf, c, r):
        x = buf[c, r + 1, PAD : PAD + C, :]
        return x, [
            buf[c, r + 1, PAD - 1 : PAD + C - 1, :],
            buf[c, r + 1, PAD + 1 : PAD + C + 1, :],
            buf[c, r, PAD : PAD + C, :],
            buf[c, r + 2, PAD : PAD + C, :],
            pltpu.roll(x, 1, 1),
            pltpu.roll(x, LAT - 1, 1),
        ]

    def setup(r, carry):
        v, vn = near(W0, 4, r)
        vn[4] = jnp.where(first, 0.0, vn[4])
        vn[5] = jnp.where(last, 0.0, vn[5])
        coefs = [(v + item) * 0.5 for item in vn]
        diag = coefs[0] + coefs[1] + coefs[2] + coefs[3] + coefs[4] + coefs[5]
        inv = 0.8 / diag
        coefs[4] = jnp.where(first, 0.0, coefs[4])
        coefs[5] = jnp.where(last, 0.0, coefs[5])
        for k in range(6):
            WT[k, r + 1, PAD : PAD + C, :] = coefs[k] * inv
        D[r] = diag * 1.25
        t, tn = near(W0, 3, r)
        tn[4] = jnp.where(first, 0.0, tn[4])
        tn[5] = jnp.where(last, 0.0, tn[5])
        advect = vel_ref[0, r] * (tn[3] - tn[2]) + vel_ref[1, r] * (tn[1] - tn[0]) + vel_ref[2, r] * (tn[5] - tn[4])
        spread = tn[0] + tn[1] + tn[2] + tn[3] + tn[4] + tn[5] - 6.0 * t
        t_next = t + 0.125 * advect + 0.1 * spread
        tn_ref[r] = t_next
        B[0, r] = (mis_ref[0, r] + t_next) * inv
        B[1, r] = mis_ref[1, r] * inv
        B[2, r] = mis_ref[2, r] * inv
        return carry

    lax.fori_loop(0, R, setup, 0)

    @pl.when(j == 0)
    def _():
        WT[2, 1] = jnp.zeros_like(WT[2, 1])

    @pl.when(j == nj - 1)
    def _():
        WT[3, R] = jnp.zeros_like(WT[3, R])

    def change(buf, c, r):
        x, xn = near(buf, c, r)
        t = B[c, r] - 0.8 * x
        for k in range(6):
            t = t + WT[k, r + 1, PAD : PAD + C, :] * xn[k]
        return x, t

    def sweep(src, dst):
        def body(r, carry):
            for c in range(3):
                x, t = change(src, c, r)
                dst[c, r + 1, PAD : PAD + C, :] = x + t
            return carry

        lax.fori_loop(0, R, body, 0)

    sweep(W0, U1)
    round1 = begin(4, U1, S.at[0], L.at[0], 3)
    round_w = begin(16, WT, SW, LW, 6)

    for item in coarse_visc:
        item.wait_recv()

    def coarse_near(buf, c, at, r, lo=PAD, width=None):
        width = width or C
        part = even[:width]
        p = 1 + half * at + r
        block = lambda place, off=0: buf[c, place, lo + off : lo + off + width, :]
        x = block(p)
        if r > 0:
            below = block(p - 1)
        else:
            below = jnp.where(part, pltpu.roll(block(p - 1), LAT - 1, 1), pltpu.roll(block(p + half - 1), 1, 1))
        if r < half - 1:
            above = block(p + 1)
        else:
            above = jnp.where(part, pltpu.roll(block(p - half + 1), LAT - 1, 1), pltpu.roll(block(p + 1), 1, 1))
        return x, [block(p, -1), block(p, 1), below, above, pltpu.roll(x, 2, 1), pltpu.roll(x, LAT - 2, 1)]

    def coarse_setup(at, carry):
        for r in range(half):
            v, vn = coarse_near(CG, 0, at, r)
            vn[4] = jnp.where(lane < 2, 0.0, vn[4])
            vn[5] = jnp.where(lane >= LAT - 2, 0.0, vn[5])
            coefs = [(v + item) * 0.5 for item in vn]
            diag = coefs[0] + coefs[1] + coefs[2] + coefs[3] + coefs[4] + coefs[5]
            inv = 0.8 / diag
            coefs[4] = jnp.where(lane < 2, 0.0, coefs[4])
            coefs[5] = jnp.where(lane >= LAT - 2, 0.0, coefs[5])
            for k in range(6):
                CW[k, half * at + r] = coefs[k] * inv
            CW[6, half * at + r] = 4.0 * inv
        return carry

    lax.fori_loop(0, nj, coarse_setup, 0)

    finish(round1, U1, L.at[0], 3)
    sweep(U1, U2)
    round2 = begin(8, U2, S.at[1], L.at[1], 3)
    finish(round2, U2, L.at[1], 3)

    def residual(q, carry):
        for c in range(3):
            x, t = change(U2, c, 2 * q)
            U3[c, 2 * q + 1, PAD : PAD + C, :] = x + t
            x, s = change(U2, c, 2 * q + 1)
            U3[c, 2 * q + 2, PAD : PAD + C, :] = x + s
            RS[c, q] = D[2 * q] * t + D[2 * q + 1] * s
        return carry

    lax.fori_loop(0, 2 * half, residual, 0)
    for c in range(3):
        pack(c, CP.at[c])
    coarse_res = gather(20 + gathers, CP, G, strip)
    round3 = begin(12, U3, S.at[2], L.at[2], 3)
    for item in coarse_res:
        item.wait_recv()

    def coarse_first(p, carry):
        for c in range(3):
            b = G[c, p + 1, PAD : PAD + C, :] * CW[6, p]
            CB[c, p] = b
            EA[c, p + 1, PAD : PAD + C, :] = b
        return carry

    lax.fori_loop(0, half * nj, coarse_first, 0)

    def coarse_sweep(src, dst, rim):
        near_rim = 2 * rim <= PAD and cols % 8 == 0
        lo = 2 * strip - PAD // 2 if near_rim else PAD
        width = cols + PAD if near_rim else C
        reach = -(-rim // (2 * half))

        def body(at, carry):
            for r in range(half):
                p = half * at + r
                for c in range(3):
                    x, xn = coarse_near(src, c, at, r, lo, width)
                    t = CB[c, p, lo - PAD : lo - PAD + width, :] + 0.2 * x
                    for k in range(6):
                        t = t + CW[k, p, lo - PAD : lo - PAD + width, :] * xn[k]
                    dst[c, p + 1, lo : lo + width, :] = t
            return carry

        lax.fori_loop(jnp.maximum(j - reach, 0), jnp.minimum(j + reach + 1, nj), body, 0)

    src, dst = EA, EB
    for number in range(NC - 1):
        coarse_sweep(src, dst, NC - 1 - number)
        src, dst = dst, src

    wide = EX.shape[2] // 2
    start = 2 * strip - PAD // 2
    even_wide = lax.rem(lax.broadcasted_iota(jnp.int32, (wide, LAT), 1), 2) == 0
    for c in range(3):
        for q in range(-1, 2 * half + 1):
            low = 0 <= q < half or q == 2 * half
            place = 1 + half * j + {-1: -1, 2 * half: half}.get(q, q % half)
            x = src[c, place, start : start + wide, :]
            if low:
                x = jnp.where(even_wide, x, pltpu.roll(x, 1, 1))
            else:
                x = jnp.where(even_wide, pltpu.roll(x, LAT - 1, 1), x)
            EX[c, q + 1, pl.ds(0, wide, 2), :] = x
            EX[c, q + 1, pl.ds(1, wide, 2), :] = x
    finish(round_w, WT, LW, 6)
    finish(round3, U3, L.at[2], 3)
    lo, hi = PAD // 2, C + PAD + PAD // 2

    for r in range(-1, R + 1):
        for c in range(3):
            x = EX[c, r // 2 + 1, lo:hi, :]
            xn = [
                EX[c, r // 2 + 1, lo - 1 : hi - 1, :],
                EX[c, r // 2 + 1, lo + 1 : hi + 1, :],
                EX[c, (r - 1) // 2 + 1, lo:hi, :],
                EX[c, (r + 1) // 2 + 1, lo:hi, :],
                pltpu.roll(x, 1, 1),
                pltpu.roll(x, LAT - 1, 1),
            ]
            t = U3[c, r + 1, lo:hi, :] + 0.2 * x
            for k in range(6):
                t = t + WT[k, r + 1, lo:hi, :] * xn[k]
            U4[c, r + 1, lo:hi, :] = t

    def closing(r, carry):
        for c in range(3):
            x, t = change(U4, c, r)
            out_ref[c, r] = x + t
        return carry

    lax.fori_loop(0, R, closing, 0)
    for item in pending:
        item.wait_send()


def deliver(tn_ref, out_ref, tn_hbm, out_hbm, sems):
    copies = [pltpu.make_async_copy(tn_ref, tn_hbm, sems.at[0]), pltpu.make_async_copy(out_ref, out_hbm, sems.at[1])]
    for item in copies:
        item.start()
    for item in copies:
        item.wait()


def solution(mesh):
    ni, nj = mesh.shape["lon"], mesh.shape["rad"]

    def local(adjoint_temp, viscosity, velocity, misfit_force, adjoint_guess):
        R, C, LAT = adjoint_temp.shape
        half, cols, wide = R // 4, C // 2, C + 2 * PAD
        f32 = jnp.float32
        frame = lambda n, rows: pltpu.VMEM((n, rows, wide, LAT), f32)
        block = lambda *dims: pltpu.VMEM(dims + (C, LAT), f32)
        copies = 20 + 2 * (3 * nj - 1)
        vmem, place = pl.BlockSpec(memory_space=pltpu.VMEM), pl.BlockSpec(memory_space=pl.ANY)
        P8 = half * nj
        results = pl.pallas_call(
            functools.partial(kernel, ni, nj),
            out_shape=(
                pltpu.VMEM(adjoint_temp.shape, f32),
                pltpu.VMEM(adjoint_guess.shape, f32),
            ),
            in_specs=[place] * 5,
            out_specs=(vmem, vmem),
            scratch_shapes=[
                block(3, R), block(3, R), pltpu.SemaphoreType.DMA((5,)),
                frame(5, R + 2), frame(3, R + 2), frame(3, R + 2), frame(3, R + 2), frame(3, R + 2),
                pltpu.VMEM((2, 6, R, LAT), f32), pltpu.VMEM((2, 6, R, LAT), f32), frame(6, R + 2), block(3, R), block(R), block(4, 2 * half),
                pltpu.VMEM((3, half, cols, LAT), f32), pltpu.VMEM((1, half, cols, LAT), f32),
                frame(3, P8 + 2), frame(1, P8 + 2), block(7, P8), block(3, P8),
                frame(3, P8 + 2), frame(3, P8 + 2), frame(3, 2 * half + 2),
                pltpu.VMEM((2, 5, R, LAT), f32), pltpu.VMEM((2, 5, R, LAT), f32),
                pltpu.VMEM((3, 2, 3, R, LAT), f32), pltpu.VMEM((3, 2, 3, R, LAT), f32),
                pltpu.SemaphoreType.DMA((copies,)), pltpu.SemaphoreType.DMA((copies,)),
            ],
            compiler_params=pltpu.CompilerParams(collective_id=0, has_side_effects=True),
        )(adjoint_temp, viscosity, velocity, misfit_force, adjoint_guess)
        return pl.pallas_call(
            deliver,
            out_shape=(jax.ShapeDtypeStruct(adjoint_temp.shape, f32), jax.ShapeDtypeStruct(adjoint_guess.shape, f32)),
            in_specs=[vmem] * 2,
            out_specs=(place, place),
            scratch_shapes=[pltpu.SemaphoreType.DMA((2,))],
        )(*[pltpu.with_memory_space_constraint(item, pltpu.VMEM) for item in results])

    flat = P("rad", "lon", None)
    full = P(None, "rad", "lon", None)
    return jax.shard_map(local, mesh=mesh, in_specs=(flat, flat, full, full, full), out_specs=(flat, full), check_vma=False)
```

```python
import functools

import jax
import jax.numpy as jnp
from jax import lax
from jax.experimental import pallas as pl
from jax.experimental.pallas import tpu as pltpu
from jax.sharding import PartitionSpec as P

NU = 2
NC = 8
PAD = 8
MESH = pl.DeviceIdType.MESH


def kernel(ni, nj, temp_hbm, visc_hbm, vel_hbm, mis_hbm, guess_hbm, tn_ref, out_ref,
           vel_ref, mis_ref, local,
           W0, U1, U2, U3, U4, SW, LW, WT, B, D, RS, CP, CV, G, CG, CW, CB, EA, EB, EX,
           S0, L0, S, L, send, recv):
    R, C, LAT = temp_hbm.shape
    half = R // 4
    cols = C // 2
    strip = PAD
    i = lax.axis_index("lon")
    j = lax.axis_index("rad")
    west, east = lax.rem(i + ni - 1, ni), lax.rem(i + 1, ni)
    down, up = lax.rem(j + nj - 1, nj), lax.rem(j + 1, nj)

    mid = pl.ds(PAD, C)
    inner = pl.ds(1, R)
    loads = [
        pltpu.make_async_copy(visc_hbm, W0.at[4, inner, mid], local.at[0]),
        pltpu.make_async_copy(temp_hbm, W0.at[3, inner, mid], local.at[1]),
        pltpu.make_async_copy(guess_hbm, W0.at[0:3, inner, mid], local.at[2]),
        pltpu.make_async_copy(vel_hbm, vel_ref, local.at[3]),
        pltpu.make_async_copy(mis_hbm, mis_ref, local.at[4]),
    ]
    for item in loads:
        item.start()

    barrier = pltpu.get_barrier_semaphore()
    for d in range(nj):
        other = lax.rem(j + d, nj)
        for lon in (west, east) if d == 0 else (west, east, i):
            pl.semaphore_signal(barrier, inc=1, device_id={"lon": lon, "rad": other}, device_id_type=MESH)

    lane = lax.broadcasted_iota(jnp.int32, (C, LAT), 1)
    first, last = lane == 0, lane == LAT - 1
    even = lax.rem(lane, 2) == 0
    even_half = even[:cols]

    def pack(slot, dst):
        for r in range(half):
            a = RS[slot, r, pl.ds(0, cols, 2), :] + RS[slot, r, pl.ds(1, cols, 2), :]
            b = RS[slot, r + half, pl.ds(0, cols, 2), :] + RS[slot, r + half, pl.ds(1, cols, 2), :]
            a = a + pltpu.roll(a, LAT - 1, 1)
            b = b + pltpu.roll(b, 1, 1)
            dst[r] = 0.125 * jnp.where(even_half, a, b)


    def copy(src, dst, slot, lon, rad):
        return pltpu.make_async_remote_copy(
            src_ref=src, dst_ref=dst, send_sem=send.at[slot], recv_sem=recv.at[slot],
            device_id={"lon": lon, "rad": rad}, device_id_type=MESH)

    pending = []

    def begin(slot, buf, stage, land, comps):
        for c in range(comps):
            stage[0, c] = buf[c, 1 : R + 1, PAD, :]
            stage[1, c] = buf[c, 1 : R + 1, PAD + C - 1, :]
        copies = [
            copy(stage.at[0], land.at[1], slot, west, j),
            copy(stage.at[1], land.at[0], slot + 1, east, j),
            copy(buf.at[:, 1, mid], buf.at[:, R + 1, mid], slot + 2, i, down),
            copy(buf.at[:, R, mid], buf.at[:, 0, mid], slot + 3, i, up),
        ]
        for item in copies:
            item.start()
        pending.extend(copies)
        return copies

    def finish(copies, buf, land, comps):
        for item in copies:
            item.wait_recv()
        for c in range(comps):
            buf[c, 1 : R + 1, PAD - 1, :] = land[0, c]
            buf[c, 1 : R + 1, PAD + C, :] = land[1, c]

    gathers = 3 * nj - 1

    def gather(slot, src, dst, width):
        copies = []
        rows = pl.ds(1 + half * j, half)
        for d in range(nj):
            other = lax.rem(j + d, nj)
            copies.append(copy(src.at[:, :, pl.ds(0, width)], dst.at[:, rows, pl.ds(2 * strip + cols, width)], slot, west, other))
            copies.append(copy(src.at[:, :, pl.ds(cols - width, width)], dst.at[:, rows, pl.ds(2 * strip - width, width)], slot + 1, east, other))
            slot = slot + 2
            if d > 0:
                copies.append(copy(src, dst.at[:, rows, pl.ds(2 * strip, cols)], slot, i, other))
                slot = slot + 1
        for item in copies:
            item.start()
        pending.extend(copies)
        for r in range(half):
            dst[:, 1 + half * j + r, 2 * strip : 2 * strip + cols, :] = src[:, r]
        return copies

    top = half * nj + 1
    for buf in (EA, EB):
        buf[...] = jnp.zeros_like(buf)
    CG[0, 0] = jnp.zeros_like(CG[0, 0])
    CG[0, top] = jnp.zeros_like(CG[0, top])

    loads[0].wait()
    for q in range(2 * half):
        RS[3, q] = W0[4, 2 * q + 1, PAD : PAD + C, :] + W0[4, 2 * q + 2, PAD : PAD + C, :]
    pack(3, CV.at[0])
    loads[1].wait()
    loads[2].wait()
    pl.semaphore_wait(barrier, gathers)

    round0 = begin(0, W0, S0, L0, 5)
    coarse_visc = gather(20, CV, CG, cols)
    loads[3].wait()
    loads[4].wait()
    finish(round0, W0, L0, 5)

    @pl.when(j == 0)
    def _():
        W0[3:5, 0] = jnp.zeros_like(W0[3:5, 0])

    @pl.when(j == nj - 1)
    def _():
        W0[3:5, R + 1] = jnp.zeros_like(W0[3:5, R + 1])

    def near(buf, c, r):
        x = buf[c, r + 1, PAD : PAD + C, :]
        return x, [
            buf[c, r + 1, PAD - 1 : PAD + C - 1, :],
            buf[c, r + 1, PAD + 1 : PAD + C + 1, :],
            buf[c, r, PAD : PAD + C, :],
            buf[c, r + 2, PAD : PAD + C, :],
            pltpu.roll(x, 1, 1),
            pltpu.roll(x, LAT - 1, 1),
        ]

    def setup(r, carry):
        v, vn = near(W0, 4, r)
        vn[4] = jnp.where(first, 0.0, vn[4])
        vn[5] = jnp.where(last, 0.0, vn[5])
        coefs = [(v + item) * 0.5 for item in vn]
        diag = coefs[0] + coefs[1] + coefs[2] + coefs[3] + coefs[4] + coefs[5]
        inv = 0.8 / diag
        coefs[4] = jnp.where(first, 0.0, coefs[4])
        coefs[5] = jnp.where(last, 0.0, coefs[5])
        for k in range(6):
            WT[k, r + 1, PAD : PAD + C, :] = coefs[k] * inv
        D[r] = diag * 1.25
        t, tn = near(W0, 3, r)
        tn[4] = jnp.where(first, 0.0, tn[4])
        tn[5] = jnp.where(last, 0.0, tn[5])
        advect = vel_ref[0, r] * (tn[3] - tn[2]) + vel_ref[1, r] * (tn[1] - tn[0]) + vel_ref[2, r] * (tn[5] - tn[4])
        spread = tn[0] + tn[1] + tn[2] + tn[3] + tn[4] + tn[5] - 6.0 * t
        t_next = t + 0.125 * advect + 0.1 * spread
        tn_ref[r] = t_next
        B[0, r] = (mis_ref[0, r] + t_next) * inv
        B[1, r] = mis_ref[1, r] * inv
        B[2, r] = mis_ref[2, r] * inv
        return carry

    lax.fori_loop(0, R, setup, 0, unroll=True)

    @pl.when(j == 0)
    def _():
        WT[2, 1] = jnp.zeros_like(WT[2, 1])

    @pl.when(j == nj - 1)
    def _():
        WT[3, R] = jnp.zeros_like(WT[3, R])

    def change(buf, c, r):
        x, xn = near(buf, c, r)
        t = B[c, r] - 0.8 * x
        for k in range(6):
            t = t + WT[k, r + 1, PAD : PAD + C, :] * xn[k]
        return x, t

    def sweep(src, dst):
        def body(r, carry):
            for c in range(3):
                x, t = change(src, c, r)
                dst[c, r + 1, PAD : PAD + C, :] = x + t
            return carry

        lax.fori_loop(0, R, body, 0, unroll=True)

    sweep(W0, U1)
    round1 = begin(4, U1, S.at[0], L.at[0], 3)
    round_w = begin(16, WT, SW, LW, 6)

    for item in coarse_visc:
        item.wait_recv()

    def coarse_near(buf, c, at, r, lo=PAD, width=None):
        width = width or C
        part = even[:width]
        p = 1 + half * at + r
        block = lambda place, off=0: buf[c, place, lo + off : lo + off + width, :]
        x = block(p)
        if r > 0:
            below = block(p - 1)
        else:
            below = jnp.where(part, pltpu.roll(block(p - 1), LAT - 1, 1), pltpu.roll(block(p + half - 1), 1, 1))
        if r < half - 1:
            above = block(p + 1)
        else:
            above = jnp.where(part, pltpu.roll(block(p - half + 1), LAT - 1, 1), pltpu.roll(block(p + 1), 1, 1))
        return x, [block(p, -1), block(p, 1), below, above, pltpu.roll(x, 2, 1), pltpu.roll(x, LAT - 2, 1)]

    def coarse_setup(at, carry):
        for r in range(half):
            v, vn = coarse_near(CG, 0, at, r)
            vn[4] = jnp.where(lane < 2, 0.0, vn[4])
            vn[5] = jnp.where(lane >= LAT - 2, 0.0, vn[5])
            coefs = [(v + item) * 0.5 for item in vn]
            diag = coefs[0] + coefs[1] + coefs[2] + coefs[3] + coefs[4] + coefs[5]
            inv = 0.8 / diag
            coefs[4] = jnp.where(lane < 2, 0.0, coefs[4])
            coefs[5] = jnp.where(lane >= LAT - 2, 0.0, coefs[5])
            for k in range(6):
                CW[k, half * at + r] = coefs[k] * inv
            CW[6, half * at + r] = 4.0 * inv
        return carry

    lax.fori_loop(0, nj, coarse_setup, 0, unroll=True)

    finish(round1, U1, L.at[0], 3)
    sweep(U1, U2)
    round2 = begin(8, U2, S.at[1], L.at[1], 3)
    finish(round2, U2, L.at[1], 3)

    def residual(q, carry):
        for c in range(3):
            x, t = change(U2, c, 2 * q)
            U3[c, 2 * q + 1, PAD : PAD + C, :] = x + t
            x, s = change(U2, c, 2 * q + 1)
            U3[c, 2 * q + 2, PAD : PAD + C, :] = x + s
            RS[c, q] = D[2 * q] * t + D[2 * q + 1] * s
        return carry

    lax.fori_loop(0, 2 * half, residual, 0, unroll=True)
    for c in range(3):
        pack(c, CP.at[c])
    coarse_res = gather(20 + gathers, CP, G, strip)
    round3 = begin(12, U3, S.at[2], L.at[2], 3)
    for item in coarse_res:
        item.wait_recv()

    def coarse_first(p, carry):
        for c in range(3):
            b = G[c, p + 1, PAD : PAD + C, :] * CW[6, p]
            CB[c, p] = b
            EA[c, p + 1, PAD : PAD + C, :] = b
        return carry

    lax.fori_loop(0, half * nj, coarse_first, 0, unroll=True)

    def coarse_sweep(src, dst, rim):
        near_rim = 2 * rim <= PAD and cols % 8 == 0
        lo = 2 * strip - PAD // 2 if near_rim else PAD
        width = cols + PAD if near_rim else C
        reach = -(-rim // (2 * half))

        def body(at, carry):
            for r in range(half):
                p = half * at + r
                for c in range(3):
                    x, xn = coarse_near(src, c, at, r, lo, width)
                    t = CB[c, p, lo - PAD : lo - PAD + width, :] + 0.2 * x
                    for k in range(6):
                        t = t + CW[k, p, lo - PAD : lo - PAD + width, :] * xn[k]
                    dst[c, p + 1, lo : lo + width, :] = t
            return carry

        if reach > 1:
            lax.fori_loop(0, nj, body, 0, unroll=True)
        else:
            lax.fori_loop(jnp.maximum(j - reach, 0), jnp.minimum(j + reach + 1, nj), body, 0)

    src, dst = EA, EB
    for number in range(NC - 1):
        coarse_sweep(src, dst, NC - 1 - number)
        src, dst = dst, src

    wide = EX.shape[2] // 2
    start = 2 * strip - PAD // 2
    even_wide = lax.rem(lax.broadcasted_iota(jnp.int32, (wide, LAT), 1), 2) == 0
    for c in range(3):
        for q in range(-1, 2 * half + 1):
            low = 0 <= q < half or q == 2 * half
            place = 1 + half * j + {-1: -1, 2 * half: half}.get(q, q % half)
            x = src[c, place, start : start + wide, :]
            if low:
                x = jnp.where(even_wide, x, pltpu.roll(x, 1, 1))
            else:
                x = jnp.where(even_wide, pltpu.roll(x, LAT - 1, 1), x)
            EX[c, q + 1, pl.ds(0, wide, 2), :] = x
            EX[c, q + 1, pl.ds(1, wide, 2), :] = x
    finish(round_w, WT, LW, 6)
    finish(round3, U3, L.at[2], 3)
    lo, hi = PAD // 2, C + PAD + PAD // 2

    for r in range(-1, R + 1):
        for c in range(3):
            x = EX[c, r // 2 + 1, lo:hi, :]
            xn = [
                EX[c, r // 2 + 1, lo - 1 : hi - 1, :],
                EX[c, r // 2 + 1, lo + 1 : hi + 1, :],
                EX[c, (r - 1) // 2 + 1, lo:hi, :],
                EX[c, (r + 1) // 2 + 1, lo:hi, :],
                pltpu.roll(x, 1, 1),
                pltpu.roll(x, LAT - 1, 1),
            ]
            t = U3[c, r + 1, lo:hi, :] + 0.2 * x
            for k in range(6):
                t = t + WT[k, r + 1, lo:hi, :] * xn[k]
            U4[c, r + 1, lo:hi, :] = t

    def closing(r, carry):
        for c in range(3):
            x, t = change(U4, c, r)
            out_ref[c, r] = x + t
        return carry

    lax.fori_loop(0, R, closing, 0, unroll=True)
    for item in pending:
        item.wait_send()


def deliver(tn_ref, out_ref, tn_hbm, out_hbm, sems):
    copies = [pltpu.make_async_copy(tn_ref, tn_hbm, sems.at[0]), pltpu.make_async_copy(out_ref, out_hbm, sems.at[1])]
    for item in copies:
        item.start()
    for item in copies:
        item.wait()


def solution(mesh):
    ni, nj = mesh.shape["lon"], mesh.shape["rad"]

    def local(adjoint_temp, viscosity, velocity, misfit_force, adjoint_guess):
        R, C, LAT = adjoint_temp.shape
        half, cols, wide = R // 4, C // 2, C + 2 * PAD
        f32 = jnp.float32
        frame = lambda n, rows: pltpu.VMEM((n, rows, wide, LAT), f32)
        block = lambda *dims: pltpu.VMEM(dims + (C, LAT), f32)
        copies = 20 + 2 * (3 * nj - 1)
        vmem, place = pl.BlockSpec(memory_space=pltpu.VMEM), pl.BlockSpec(memory_space=pl.ANY)
        P8 = half * nj
        results = pl.pallas_call(
            functools.partial(kernel, ni, nj),
            out_shape=(
                pltpu.VMEM(adjoint_temp.shape, f32),
                pltpu.VMEM(adjoint_guess.shape, f32),
            ),
            in_specs=[place] * 5,
            out_specs=(vmem, vmem),
            scratch_shapes=[
                block(3, R), block(3, R), pltpu.SemaphoreType.DMA((5,)),
                frame(5, R + 2), frame(3, R + 2), frame(3, R + 2), frame(3, R + 2), frame(3, R + 2),
                pltpu.VMEM((2, 6, R, LAT), f32), pltpu.VMEM((2, 6, R, LAT), f32), frame(6, R + 2), block(3, R), block(R), block(4, 2 * half),
                pltpu.VMEM((3, half, cols, LAT), f32), pltpu.VMEM((1, half, cols, LAT), f32),
                frame(3, P8 + 2), frame(1, P8 + 2), block(7, P8), block(3, P8),
                frame(3, P8 + 2), frame(3, P8 + 2), frame(3, 2 * half + 2),
                pltpu.VMEM((2, 5, R, LAT), f32), pltpu.VMEM((2, 5, R, LAT), f32),
                pltpu.VMEM((3, 2, 3, R, LAT), f32), pltpu.VMEM((3, 2, 3, R, LAT), f32),
                pltpu.SemaphoreType.DMA((copies,)), pltpu.SemaphoreType.DMA((copies,)),
            ],
            compiler_params=pltpu.CompilerParams(collective_id=0, has_side_effects=True),
        )(adjoint_temp, viscosity, velocity, misfit_force, adjoint_guess)
        return pl.pallas_call(
            deliver,
            out_shape=(jax.ShapeDtypeStruct(adjoint_temp.shape, f32), jax.ShapeDtypeStruct(adjoint_guess.shape, f32)),
            in_specs=[vmem] * 2,
            out_specs=(place, place),
            scratch_shapes=[pltpu.SemaphoreType.DMA((2,))],
        )(*[pltpu.with_memory_space_constraint(item, pltpu.VMEM) for item in results])

    flat = P("rad", "lon", None)
    full = P(None, "rad", "lon", None)
    return jax.shard_map(local, mesh=mesh, in_specs=(flat, flat, full, full, full), out_specs=(flat, full), check_vma=False)
```
